32 devices in a mesh: row: 8 (over z, x), col: 4 (over y, core).
Axes of the slice: x: 2, y: 2, z: 4, core: 2. Of those that a mesh axis runs over, the one named last changes fastest.
Arguments:
- diagonal: float32 [32, 512, 512], P(('row', 'col')), may hold values from -0.05 to 1.05
- lower: float32 [32, 512, 512], P(('row', 'col')), may hold values from -1 to 1, as said below
- upper: float32 [32, 512, 512], P(('row', 'col')), may hold values from -1 to 1, as said below
- right_side: float32 [32, 512, 128], P(('row', 'col')), may hold values from -6 to 6
- guess: float32 [32, 512, 128], P(('row', 'col')), may hold values from -4 to 4
Outputs:
- solution: float32 [32, 512, 128], P(('row', 'col'))
The draws below stay inside these ranges and needn't reach their ends.
Inputs may be any that keep to these rules, and one draw needn't show every extreme that they name: `lower`: each block is one half of an orthogonal matrix. `upper`: each block is one half of an orthogonal matrix.
All inputs are finite; a program needn't handle non-finite values.
Results may differ from the reference program's by a relative error of at most 0.00026.
Values sent between devices are 32-bit elements; how exact they have to be, the bound alone decides.
A program may use at most 64 MiB of HBM per device.

```python
import jax
import jax.numpy as jnp
from jax import lax

B = 512
R = 128
LEVELS = 2
NEWTON = 2
NB = 32


def draw_diagonal(key, part):
    scale = 0.025 / B ** 0.5
    shift_key = jax.random.fold_in(key, 5)
    noise_key = jax.random.fold_in(key, 7)
    shift = jax.random.uniform(shift_key, (NB,), jnp.float32, 1.004, 1.009)
    noise = jnp.clip(jax.random.normal(noise_key, (NB, B, B), jnp.float32), -6.0, 6.0) * scale
    return shift[:, None, None] * jnp.eye(B, dtype=jnp.float32) + noise


def half_orthogonal(key):
    gauss = jax.random.normal(key, (NB, B, B), jnp.float32)
    basis, upper_tri = jnp.linalg.qr(gauss)
    signs = jnp.sign(jnp.diagonal(upper_tri, axis1=1, axis2=2)) + (jnp.diagonal(upper_tri, axis1=1, axis2=2) == 0)
    return 0.5 * basis * signs[:, None, :]


def coupling_basis(key):
    return half_orthogonal(jax.random.fold_in(key, 11))


def draw_lower(key, part):
    return -coupling_basis(key)


def draw_upper(key, part):
    following = jnp.roll(coupling_basis(key), -1, axis=0)
    return -jnp.swapaxes(following, 1, 2)


def level_of(key, shape, shards, smallest, largest):
    def one(dim, blocks):
        heights = jax.random.uniform(jax.random.fold_in(jax.random.fold_in(key, 6), dim), (blocks,), jnp.float32, smallest / len(shards), largest / len(shards))
        return jnp.repeat(jnp.exp(heights), shape[dim] // blocks).reshape((-1,) + (1,) * (len(shape) - dim - 1))

    factor_of = one(*shards[0])
    for cut in shards[1:]:
        factor_of = factor_of * one(*cut)
    return factor_of


def scatter_about(stream_key, extent, deviation, most, cuts=(), held_as=jnp.bfloat16):
    drawn = jax.random.normal(stream_key, extent, jnp.float32) * deviation
    if len(cuts) > 0:
        drawn = level_of(stream_key, extent, cuts, -0.22, 0.18) * drawn
    return jnp.clip(drawn, min=-most, max=most).astype(held_as)


def setup_inputs(seed: int = 0) -> dict:
    streams_of = jax.random.split(jax.random.key(seed), 6)
    return {
        "diagonal": draw_diagonal(jax.random.fold_in(streams_of[5], 71), 0),
        "lower": draw_lower(jax.random.fold_in(streams_of[5], 71), 0),
        "upper": draw_upper(jax.random.fold_in(streams_of[5], 71), 0),
        "right_side": scatter_about(streams_of[3], (NB, B, R), 1.0, 6.0, ((0, 32),), jnp.float32),
        "guess": scatter_about(streams_of[4], (NB, B, R), 1.0, 4.0, ((0, 32),), jnp.float32),
    }


def multiply(left, right):
    return jnp.matmul(left, right, precision=lax.Precision.HIGHEST)

def invert(matrix):
    order = matrix.shape[-1]
    eye = jnp.eye(order, dtype=jnp.float32)
    mean_diag = jnp.trace(matrix, axis1=-2, axis2=-1) / order
    approx = eye / mean_diag[..., None, None]
    for step in range(NEWTON):
        approx = multiply(approx, 2.0 * eye - multiply(matrix, approx))
    return approx

def from_before(array, stride):
    return jnp.concatenate([jnp.zeros_like(array[:stride]), array[:-stride]], axis=0)

def from_after(array, stride):
    return jnp.concatenate([array[stride:], jnp.zeros_like(array[:stride])], axis=0)

def reference(diagonal, lower, upper, right_side, guess):
    count = diagonal.shape[0]
    rows = jnp.arange(count, dtype=jnp.int32)[:, None, None]
    low = jnp.where(rows == 0, jnp.float32(0.0), lower)
    up = jnp.where(rows == count - 1, jnp.float32(0.0), upper)
    diag = diagonal
    rhs = right_side
    for level in range(LEVELS):
        stride = 2 ** level
        pivot = invert(diag)
        scaled_low = multiply(pivot, low)
        scaled_up = multiply(pivot, up)
        scaled_rhs = multiply(pivot, rhs)
        new_diag = diag - multiply(low, from_before(scaled_up, stride)) - multiply(up, from_after(scaled_low, stride))
        new_rhs = rhs - multiply(low, from_before(scaled_rhs, stride)) - multiply(up, from_after(scaled_rhs, stride))
        new_low = -multiply(low, from_before(scaled_low, stride))
        new_up = -multiply(up, from_after(scaled_up, stride))
        diag, low, up, rhs = (new_diag, new_low, new_up, new_rhs)
    reach = 2 ** LEVELS
    inner = rhs - multiply(low, from_before(guess, reach)) - multiply(up, from_after(guess, reach))
    return multiply(invert(diag), inner)
```

```python
import jax
import jax.numpy as jnp
from jax import lax
from jax.sharding import PartitionSpec as P

AXES = ("row", "col")


def multiply(left, right):
    return jnp.dot(left, right, precision=lax.Precision.HIGH, preferred_element_type=jnp.float32)


def permuted(value, pairs, chain):
    kept = [(s, d) for s, d in pairs if 0 <= d < chain]
    return lax.ppermute(value, AXES, kept)


def first_step(matrix):
    order = matrix.shape[-1]
    eye = jnp.eye(order, dtype=jnp.float32)
    t = jnp.trace(matrix) / order
    return (2.0 * eye - matrix / t) / t, eye, t


def invert(matrix):
    approx, eye, _ = first_step(matrix)
    return multiply(approx, 2.0 * eye - multiply(matrix, approx))


def apply_inverse(matrix, value):
    t = jnp.trace(matrix) / matrix.shape[-1]

    def first(v):
        return (2.0 * v - multiply(matrix, v) / t) / t

    return first(2.0 * value - multiply(matrix, first(value)))


def body(diagonal, lower, upper, right_side, guess):
    chain = lax.axis_size("row") * lax.axis_size("col")
    place = lax.axis_index("row") * lax.axis_size("col") + lax.axis_index("col")
    even = place % 2 == 0
    diag, rhs, g = diagonal[0], right_side[0], guess[0]
    order = diag.shape[0]
    inward = jnp.where(even, upper[0], lower[0])
    edge = (place == 0) | (place == chain - 1)
    outward = jnp.where(edge, jnp.float32(0.0), jnp.where(even, lower[0], upper[0]))

    rows = range(chain)
    partner = [(i, i ^ 1) for i in rows]
    outer = [(i, i - 1 if i % 2 == 0 else i + 1) for i in rows]
    to_out = [(i, i - 2 if i % 2 == 0 else i + 2) for i in rows]
    to_in = [(i, i + 2 if i % 2 == 0 else i - 2) for i in rows]

    g_o = permuted(g, outer, chain)
    g_p = permuted(g, partner, chain)
    pivot = invert(diag)
    s_out = multiply(pivot, outward)
    so_o = permuted(s_out, outer, chain)
    s_in = multiply(pivot, inward)
    s_b = multiply(pivot, rhs)
    b_o, q_o = permuted((s_b, multiply(s_in, g_p)), outer, chain)
    si_p, so_p, b_p, h_p = permuted((s_in, s_out, s_b, multiply(s_out, g_o)), partner, chain)
    diag1 = diag - multiply(inward, si_p) - multiply(outward, so_o)
    rhs1 = rhs - multiply(inward, b_p) - multiply(outward, b_o)
    in1 = -multiply(inward, so_p)
    pivot = invert(diag1)
    h = multiply(pivot, outward)
    r_h = permuted(h, to_out, chain)
    r_g = permuted(multiply(si_p, multiply(pivot, in1)), to_in, chain)
    w_h = multiply(pivot, rhs1 + multiply(inward, h_p))
    w_g = multiply(si_p, multiply(pivot, rhs1 + multiply(outward, q_o)))
    r_wh = permuted(w_h, to_out, chain)
    r_wg = permuted(w_g, to_in, chain)
    diag2 = diag1 + multiply(multiply(in1, r_h), si_p) + multiply(outward, r_g)
    inner = rhs1 + multiply(outward, r_wg) - multiply(in1, r_wh)
    return apply_inverse(diag2, inner)[None]


def solution(mesh):
    spec = P(AXES, None, None)
    return jax.shard_map(body, mesh=mesh, in_specs=(spec,) * 5, out_specs=spec, check_vma=False)
```

```python
import functools
from collections import namedtuple

import jax
import jax.numpy as jnp
from jax import lax
from jax.experimental import pallas as pl
from jax.experimental.pallas import tpu as pltpu
from jax.sharding import PartitionSpec as P

AXES = ("row", "col")
F32, BF16 = jnp.float32, jnp.bfloat16
CHUNKS = 2

MESSAGES = (
    ("g_outer", 1), ("g_partner", 1),
    ("so_outer", CHUNKS), ("so_partner", CHUNKS), ("si_partner", CHUNKS),
    ("b_outer", 1), ("b_partner", 1), ("q_outer", 1), ("v_partner", 1),
    ("h_out", CHUNKS), ("wh_out", 1), ("g_in", CHUNKS), ("wg_in", 1),
)
FIRST = {}
for _name, _count in MESSAGES:
    FIRST[_name] = sum(count for _, count in MESSAGES[: len(FIRST)])
TOTAL = sum(count for _, count in MESSAGES)


def scratch_types(order, columns):
    matrix = pltpu.VMEM((order, order), F32)
    chunked = pltpu.VMEM((CHUNKS, order, order // CHUNKS), F32)
    vector = pltpu.VMEM((order, columns), F32)
    pair = pltpu.VMEM((2, order, order), BF16)
    vector_pair = pltpu.VMEM((2, order, columns), BF16)
    types = dict(diag=matrix, l_in=matrix, l_out=matrix, rhs=vector)
    types.update({name: chunked for name in ("s_out", "s_in", "h_mat", "g_mat")})
    types.update({name: vector for name in ("s_b", "q_vec", "v_vec", "wh", "wg", "via")})
    types.update({f"r_{name}": chunked if count > 1 else vector for name, count in MESSAGES})
    types.update({name: pair for name in ("d2", "x2", "y2", "p2", "lin2", "lout2", "sin2", "sout2", "sip2", "in2", "t2", "u2", "k2")})
    types.update(vec2=vector_pair)
    types.update(load_sem=pltpu.SemaphoreType.DMA((4,)))
    types.update(send_sem=pltpu.SemaphoreType.DMA((TOTAL,)), recv_sem=pltpu.SemaphoreType.DMA((TOTAL,)))
    return types


def kernel(chain, across, names, d_hbm, low_hbm, up_hbm, b_hbm, g_hbm, out_ref, *scratch):
    s = namedtuple("Scratch", names)(*scratch)
    order = s.diag.shape[0]
    width = order // CHUNKS
    place = lax.axis_index("row") * across + lax.axis_index("col")
    odd = lax.rem(place, 2)
    even = odd == 0
    step = 1 - 2 * odd
    inside = (place > 0) & (place < chain - 1)
    edge = (place == 0) | (place == chain - 1)
    deep = (place != 1) & (place != chain - 2)
    shallow = (place == 1) | (place == chain - 2)

    def device(offset):
        index = lax.rem(place + offset * step + chain, chain)
        return (index // across, lax.rem(index, across))

    peers = {"partner": device(1), "outer": device(-1), "out": device(-2), "in": device(2)}
    sent_if = {"partner": None, "outer": inside, "out": inside, "in": deep}
    came_if = {"partner": None, "outer": inside, "out": deep, "in": inside}

    def guarded(condition, action):
        if condition is None:
            action()
        else:
            pl.when(condition)(action)

    def copy(name, src, chunk):
        dst = getattr(s, "r_" + name)
        index = FIRST[name] + chunk
        if dst.ndim == 3:
            dst = dst.at[chunk]
        return pltpu.make_async_remote_copy(
            src_ref=src if src is not None else dst,
            dst_ref=dst,
            send_sem=s.send_sem.at[index],
            recv_sem=s.recv_sem.at[index],
            device_id=peers[name.split("_")[1]],
            device_id_type=pl.DeviceIdType.MESH,
        )

    pending = []

    def send(name, src, chunk=0):
        guarded(sent_if[name.split("_")[1]], lambda: copy(name, src, chunk).start())
        pending.append((name, src, chunk))

    def receive(name, chunk=0):
        guarded(came_if[name.split("_")[1]], lambda: copy(name, None, chunk).wait_recv())

    def load(src, dst, index):
        return pltpu.make_async_copy(src.at[0], dst, s.load_sem.at[index])

    def load_out(act):
        pl.when(inside & even)(lambda: act(load(low_hbm, s.l_out, 1)))
        pl.when(inside & (odd == 1))(lambda: act(load(up_hbm, s.l_out, 1)))

    def load_in(act):
        pl.when(even)(lambda: act(load(up_hbm, s.l_in, 2)))
        pl.when(odd == 1)(lambda: act(load(low_hbm, s.l_in, 2)))

    load(d_hbm, s.diag, 0).start()
    load_out(lambda c: c.start())
    load_in(lambda c: c.start())
    load(b_hbm, s.rhs, 3).start()

    barrier = pltpu.get_barrier_semaphore()
    for side in ("partner", "outer", "out", "in"):
        guarded(sent_if[side], lambda: pl.semaphore_signal(
            barrier, inc=1, device_id=peers[side], device_id_type=pl.DeviceIdType.MESH))
    pl.semaphore_wait(barrier, 1 + jnp.where(inside, 2, 0) + jnp.where(deep, 1, 0))

    send("g_outer", g_hbm.at[0])
    send("g_partner", g_hbm.at[0])

    def zero(*refs):
        for ref in refs:
            ref[...] = jnp.zeros_like(ref)

    pl.when(edge)(lambda: zero(s.l_out, s.r_g_outer, s.r_so_outer, s.r_b_outer, s.r_q_outer, s.r_g_in, s.r_wg_in))
    pl.when(shallow)(lambda: zero(s.r_h_out, s.r_wh_out))

    def cols(chunk):
        return slice(chunk * width, (chunk + 1) * width)

    def put(pair, value, where=slice(None)):
        high = value.astype(BF16)
        pair[0, :, where] = high
        pair[1, :, where] = (value - high.astype(F32)).astype(BF16)

    def dot(left, right):
        return jnp.dot(left, right, preferred_element_type=F32)

    def multiply(left, right, where=slice(None)):
        high, low = right[0, :, where], right[1, :, where]
        return dot(left[0], high) + (dot(left[0], low) + dot(left[1], high))

    def eye(chunk):
        rows = lax.broadcasted_iota(jnp.int32, (order, width), 0)
        return (rows == lax.broadcasted_iota(jnp.int32, (order, width), 1) + chunk * width).astype(F32)

    def mean_diag():
        total = jnp.float32(0.0)
        for c in range(CHUNKS):
            total += jnp.sum(eye(c) * s.diag[:, cols(c)])
        return total / order

    def invert():
        scale = 1.0 / mean_diag()
        for c in range(CHUNKS):
            block = s.diag[:, cols(c)]
            put(s.d2, block, cols(c))
            put(s.x2, (2.0 * eye(c) - block * scale) * scale, cols(c))
        for c in range(CHUNKS):
            put(s.y2, 2.0 * eye(c) - multiply(s.d2, s.x2, cols(c)), cols(c))
        for c in range(CHUNKS):
            put(s.p2, multiply(s.x2, s.y2, cols(c)), cols(c))

    def times(left, vector):
        put(s.vec2, vector)
        return multiply(left, s.vec2)

    load(d_hbm, s.diag, 0).wait()
    invert()
    load_out(lambda c: c.wait())
    put(s.lout2, s.l_out[...])
    for c in range(CHUNKS):
        block = multiply(s.p2, s.lout2, cols(c))
        s.s_out[c] = block
        send("so_outer", s.s_out.at[c], c)
        send("so_partner", s.s_out.at[c], c)
        put(s.sout2, block, cols(c))
    load(b_hbm, s.rhs, 3).wait()
    s.s_b[...] = times(s.p2, s.rhs[...])
    send("b_outer", s.s_b)
    send("b_partner", s.s_b)
    load_in(lambda c: c.wait())
    put(s.lin2, s.l_in[...])
    for c in range(CHUNKS):
        block = multiply(s.p2, s.lin2, cols(c))
        s.s_in[c] = block
        send("si_partner", s.s_in.at[c], c)
        put(s.sin2, block, cols(c))
    receive("g_partner")
    s.q_vec[...] = times(s.sin2, s.r_g_partner[...])
    send("q_outer", s.q_vec)
    receive("g_outer")
    s.v_vec[...] = times(s.sout2, s.r_g_outer[...])
    send("v_partner", s.v_vec)

    for c in range(CHUNKS):
        receive("si_partner", c)
        put(s.sip2, s.r_si_partner[c], cols(c))
        s.diag[:, cols(c)] = s.diag[:, cols(c)] - multiply(s.lin2, s.sip2, cols(c))
    for c in range(CHUNKS):
        receive("so_partner", c)
        put(s.t2, s.r_so_partner[c], cols(c))
        put(s.in2, -multiply(s.lin2, s.t2, cols(c)), cols(c))
    receive("b_partner")
    s.rhs[...] = s.rhs[...] - times(s.lin2, s.r_b_partner[...])
    receive("v_partner")
    s.via[...] = times(s.lin2, s.r_v_partner[...])
    for c in range(CHUNKS):
        receive("so_outer", c)
        put(s.u2, s.r_so_outer[c], cols(c))
        s.diag[:, cols(c)] = s.diag[:, cols(c)] - multiply(s.lout2, s.u2, cols(c))

    invert()
    for c in range(CHUNKS):
        s.h_mat[c] = multiply(s.p2, s.lout2, cols(c))
        send("h_out", s.h_mat.at[c], c)
    receive("b_outer")
    s.rhs[...] = s.rhs[...] - times(s.lout2, s.r_b_outer[...])
    s.wh[...] = times(s.p2, s.rhs[...] + s.via[...])
    send("wh_out", s.wh)
    for c in range(CHUNKS):
        put(s.k2, multiply(s.sip2, s.p2, cols(c)), cols(c))
    for c in range(CHUNKS):
        s.g_mat[c] = multiply(s.k2, s.in2, cols(c))
        send("g_in", s.g_mat.at[c], c)
    receive("q_outer")
    s.wg[...] = times(s.k2, s.rhs[...] + times(s.lout2, s.r_q_outer[...]))
    send("wg_in", s.wg)

    for c in range(CHUNKS):
        receive("h_out", c)
        put(s.t2, s.r_h_out[c], cols(c))
        put(s.u2, multiply(s.in2, s.t2, cols(c)), cols(c))
    for c in range(CHUNKS):
        s.diag[:, cols(c)] = s.diag[:, cols(c)] + multiply(s.u2, s.sip2, cols(c))
    receive("wh_out")
    s.rhs[...] = s.rhs[...] - times(s.in2, s.r_wh_out[...])
    for c in range(CHUNKS):
        receive("g_in", c)
        put(s.t2, s.r_g_in[c], cols(c))
        block = s.diag[:, cols(c)] + multiply(s.lout2, s.t2, cols(c))
        s.diag[:, cols(c)] = block
        put(s.d2, block, cols(c))
    scale = 1.0 / mean_diag()
    receive("wg_in")
    inner = s.rhs[...] + times(s.lout2, s.r_wg_in[...])

    half = (2.0 * inner - times(s.d2, inner) * scale) * scale
    rest = 2.0 * inner - times(s.d2, half)
    out_ref[...] = (2.0 * rest - times(s.d2, rest) * scale) * scale

    for name, src, chunk in pending:
        guarded(sent_if[name.split("_")[1]], lambda: copy(name, src, chunk).wait_send())


def body(diagonal, lower, upper, right_side, guess):
    across = lax.axis_size("col")
    chain = lax.axis_size("row") * across
    order, columns = right_side.shape[1:]
    types = scratch_types(order, columns)
    result = pl.pallas_call(
        functools.partial(kernel, chain, across, tuple(types)),
        out_shape=jax.ShapeDtypeStruct((order, columns), F32),
        in_specs=[pl.BlockSpec(memory_space=pl.ANY)] * 5,
        out_specs=pl.BlockSpec(memory_space=pltpu.VMEM),
        scratch_shapes=list(types.values()),
        compiler_params=pltpu.CompilerParams(collective_id=0, has_side_effects=True),
    )(diagonal, lower, upper, right_side, guess)
    return result[None]


def solution(mesh):
    spec = P(AXES, None, None)
    return jax.shard_map(body, mesh=mesh, in_specs=(spec,) * 5, out_specs=spec, check_vma=False)
```

```python
import functools
from collections import namedtuple

import jax
import jax.numpy as jnp
from jax import lax
from jax.experimental import pallas as pl
from jax.experimental.pallas import tpu as pltpu
from jax.sharding import PartitionSpec as P

AXES = ("row", "col")
F32, BF16 = jnp.float32, jnp.bfloat16
CHUNKS = 2

MESSAGES = (
    ("g_outer", 1), ("g_partner", 1),
    ("so_outer", CHUNKS), ("so_partner", CHUNKS), ("si_partner", CHUNKS),
    ("b_partner", 1), ("e_outer", 1), ("v_partner", 1),
    ("h_out", CHUNKS), ("wh_out", 1), ("g_in", CHUNKS), ("wg_in", 1),
)
FIRST = {}
for _name, _count in MESSAGES:
    FIRST[_name] = sum(count for _, count in MESSAGES[: len(FIRST)])
TOTAL = sum(count for _, count in MESSAGES)


def scratch_types(order, columns):
    matrix = pltpu.VMEM((order, order), F32)
    chunked = pltpu.VMEM((CHUNKS, order, order // CHUNKS), F32)
    vector = pltpu.VMEM((order, columns), F32)
    pair = pltpu.VMEM((2, order, order), BF16)
    vector_pair = pltpu.VMEM((2, order, columns), BF16)
    types = dict(diag=matrix, l_in=matrix, l_out=matrix, rhs=vector)
    types.update({name: chunked for name in ("s_out", "s_in", "h_mat", "g_mat")})
    types.update({name: vector for name in ("s_b", "e_vec", "v_vec", "wh", "wg", "via")})
    types.update({f"r_{name}": chunked if count > 1 else vector for name, count in MESSAGES})
    types.update({name: pair for name in ("d2", "x2", "y2", "p2", "lin2", "lout2", "sin2", "sout2", "sip2", "in2", "t2", "u2", "k2")})
    types.update(vec2=vector_pair, bp2=vector_pair)
    types.update(load_sem=pltpu.SemaphoreType.DMA((4,)))
    types.update(send_sem=pltpu.SemaphoreType.DMA((TOTAL,)), recv_sem=pltpu.SemaphoreType.DMA((TOTAL,)))
    return types


def kernel(chain, across, names, d_hbm, low_hbm, up_hbm, b_hbm, g_hbm, out_ref, *scratch):
    s = namedtuple("Scratch", names)(*scratch)
    order = s.diag.shape[0]
    width = order // CHUNKS
    place = lax.axis_index("row") * across + lax.axis_index("col")
    odd = lax.rem(place, 2)
    even = odd == 0
    step = 1 - 2 * odd
    inside = (place > 0) & (place < chain - 1)
    edge = (place == 0) | (place == chain - 1)
    deep = (place != 1) & (place != chain - 2)
    shallow = (place == 1) | (place == chain - 2)

    def device(offset):
        index = lax.rem(place + offset * step + chain, chain)
        return (index // across, lax.rem(index, across))

    peers = {"partner": device(1), "outer": device(-1), "out": device(-2), "in": device(2)}
    sent_if = {"partner": None, "outer": inside, "out": inside, "in": deep}
    came_if = {"partner": None, "outer": inside, "out": deep, "in": inside}

    def guarded(condition, action):
        if condition is None:
            action()
        else:
            pl.when(condition)(action)

    def copy(name, src, chunk):
        dst = getattr(s, "r_" + name)
        index = FIRST[name] + chunk
        if dst.ndim == 3:
            dst = dst.at[chunk]
        return pltpu.make_async_remote_copy(
            src_ref=src if src is not None else dst,
            dst_ref=dst,
            send_sem=s.send_sem.at[index],
            recv_sem=s.recv_sem.at[index],
            device_id=peers[name.split("_")[1]],
            device_id_type=pl.DeviceIdType.MESH,
        )

    pending = []

    def send(name, src, chunk=0):
        guarded(sent_if[name.split("_")[1]], lambda: copy(name, src, chunk).start())
        pending.append((name, src, chunk))

    def receive(name, chunk=0):
        guarded(came_if[name.split("_")[1]], lambda: copy(name, None, chunk).wait_recv())

    def load(src, dst, index):
        return pltpu.make_async_copy(src.at[0], dst, s.load_sem.at[index])

    def load_out(act):
        pl.when(inside & even)(lambda: act(load(low_hbm, s.l_out, 1)))
        pl.when(inside & (odd == 1))(lambda: act(load(up_hbm, s.l_out, 1)))

    def load_in(act):
        pl.when(even)(lambda: act(load(up_hbm, s.l_in, 2)))
        pl.when(odd == 1)(lambda: act(load(low_hbm, s.l_in, 2)))

    load(d_hbm, s.diag, 0).start()
    load_out(lambda c: c.start())
    load_in(lambda c: c.start())
    load(b_hbm, s.rhs, 3).start()

    barrier = pltpu.get_barrier_semaphore()
    for side in ("partner", "outer", "out", "in"):
        guarded(sent_if[side], lambda: pl.semaphore_signal(
            barrier, inc=1, device_id=peers[side], device_id_type=pl.DeviceIdType.MESH))
    pl.semaphore_wait(barrier, 1 + jnp.where(inside, 2, 0) + jnp.where(deep, 1, 0))

    send("g_outer", g_hbm.at[0])
    send("g_partner", g_hbm.at[0])

    def zero(*refs):
        for ref in refs:
            ref[...] = jnp.zeros_like(ref)

    pl.when(edge)(lambda: zero(s.l_out, s.r_g_outer, s.r_so_outer, s.r_e_outer, s.r_g_in, s.r_wg_in))
    pl.when(shallow)(lambda: zero(s.r_h_out, s.r_wh_out))

    def cols(chunk):
        return slice(chunk * width, (chunk + 1) * width)

    def put(pair, value, where=slice(None)):
        high = value.astype(BF16)
        pair[0, :, where] = high
        pair[1, :, where] = (value - high.astype(F32)).astype(BF16)

    def dot(left, right):
        return jnp.dot(left, right, preferred_element_type=F32)

    def multiply(left, right, where=slice(None)):
        high, low = right[0, :, where], right[1, :, where]
        return dot(left[0], high) + (dot(left[0], low) + dot(left[1], high))

    def eye(chunk):
        rows = lax.broadcasted_iota(jnp.int32, (order, width), 0)
        return (rows == lax.broadcasted_iota(jnp.int32, (order, width), 1) + chunk * width).astype(F32)

    def mean_diag():
        total = jnp.float32(0.0)
        for c in range(CHUNKS):
            total += jnp.sum(eye(c) * s.diag[:, cols(c)])
        return total / order

    def invert():
        scale = 1.0 / mean_diag()
        for c in range(CHUNKS):
            block = s.diag[:, cols(c)]
            put(s.d2, block, cols(c))
            put(s.x2, (2.0 * eye(c) - block * scale) * scale, cols(c))
        for c in range(CHUNKS):
            put(s.y2, 2.0 * eye(c) - multiply(s.d2, s.x2, cols(c)), cols(c))
        for c in range(CHUNKS):
            put(s.p2, multiply(s.x2, s.y2, cols(c)), cols(c))

    def times(left, vector):
        put(s.vec2, vector)
        return multiply(left, s.vec2)

    load(d_hbm, s.diag, 0).wait()
    invert()
    load_out(lambda c: c.wait())
    put(s.lout2, s.l_out[...])
    for c in range(CHUNKS):
        block = multiply(s.p2, s.lout2, cols(c))
        s.s_out[c] = block
        send("so_outer", s.s_out.at[c], c)
        send("so_partner", s.s_out.at[c], c)
        put(s.sout2, block, cols(c))
    load(b_hbm, s.rhs, 3).wait()
    s.s_b[...] = times(s.p2, s.rhs[...])
    send("b_partner", s.s_b)
    load_in(lambda c: c.wait())
    put(s.lin2, s.l_in[...])
    for c in range(CHUNKS):
        block = multiply(s.p2, s.lin2, cols(c))
        s.s_in[c] = block
        send("si_partner", s.s_in.at[c], c)
        put(s.sin2, block, cols(c))
    receive("g_partner")
    s.e_vec[...] = s.s_b[...] - times(s.sin2, s.r_g_partner[...])
    send("e_outer", s.e_vec)
    receive("g_outer")
    s.v_vec[...] = times(s.sout2, s.r_g_outer[...])
    send("v_partner", s.v_vec)

    for c in range(CHUNKS):
        receive("si_partner", c)
        put(s.sip2, s.r_si_partner[c], cols(c))
        s.diag[:, cols(c)] = s.diag[:, cols(c)] - multiply(s.lin2, s.sip2, cols(c))
    for c in range(CHUNKS):
        receive("so_partner", c)
        put(s.t2, s.r_so_partner[c], cols(c))
        put(s.in2, -multiply(s.lin2, s.t2, cols(c)), cols(c))
    receive("b_partner")
    put(s.bp2, s.r_b_partner[...])
    s.rhs[...] = s.rhs[...] - multiply(s.lin2, s.bp2)
    receive("v_partner")
    s.via[...] = times(s.lin2, s.r_v_partner[...])
    for c in range(CHUNKS):
        receive("so_outer", c)
        put(s.u2, s.r_so_outer[c], cols(c))
        s.diag[:, cols(c)] = s.diag[:, cols(c)] - multiply(s.lout2, s.u2, cols(c))

    invert()
    for c in range(CHUNKS):
        s.h_mat[c] = multiply(s.p2, s.lout2, cols(c))
        send("h_out", s.h_mat.at[c], c)
    s.wh[...] = times(s.p2, s.rhs[...] + s.via[...])
    send("wh_out", s.wh)
    for c in range(CHUNKS):
        put(s.k2, multiply(s.sip2, s.p2, cols(c)), cols(c))
    for c in range(CHUNKS):
        s.g_mat[c] = multiply(s.k2, s.in2, cols(c))
        send("g_in", s.g_mat.at[c], c)
    receive("e_outer")
    s.wg[...] = times(s.k2, s.rhs[...] - times(s.lout2, s.r_e_outer[...])) - s.r_b_partner[...]
    send("wg_in", s.wg)

    for c in range(CHUNKS):
        receive("h_out", c)
        put(s.t2, s.r_h_out[c], cols(c))
        put(s.u2, multiply(s.in2, s.t2, cols(c)), cols(c))
    for c in range(CHUNKS):
        s.diag[:, cols(c)] = s.diag[:, cols(c)] + multiply(s.u2, s.sip2, cols(c))
    receive("wh_out")
    s.rhs[...] = s.rhs[...] - times(s.in2, s.r_wh_out[...] - multiply(s.t2, s.bp2))
    for c in range(CHUNKS):
        receive("g_in", c)
        put(s.t2, s.r_g_in[c], cols(c))
        block = s.diag[:, cols(c)] + multiply(s.lout2, s.t2, cols(c))
        s.diag[:, cols(c)] = block
        put(s.d2, block, cols(c))
    scale = 1.0 / mean_diag()
    receive("wg_in")
    inner = s.rhs[...] + times(s.lout2, s.r_wg_in[...])

    half = (2.0 * inner - times(s.d2, inner) * scale) * scale
    rest = 2.0 * inner - times(s.d2, half)
    out_ref[...] = (2.0 * rest - times(s.d2, rest) * scale) * scale

    for name, src, chunk in pending:
        guarded(sent_if[name.split("_")[1]], lambda: copy(name, src, chunk).wait_send())


def body(diagonal, lower, upper, right_side, guess):
    across = lax.axis_size("col")
    chain = lax.axis_size("row") * across
    order, columns = right_side.shape[1:]
    types = scratch_types(order, columns)
    result = pl.pallas_call(
        functools.partial(kernel, chain, across, tuple(types)),
        out_shape=jax.ShapeDtypeStruct((order, columns), F32),
        in_specs=[pl.BlockSpec(memory_space=pl.ANY)] * 5,
        out_specs=pl.BlockSpec(memory_space=pltpu.VMEM),
        scratch_shapes=list(types.values()),
        compiler_params=pltpu.CompilerParams(collective_id=0, has_side_effects=True),
    )(diagonal, lower, upper, right_side, guess)
    return result[None]


def solution(mesh):
    spec = P(AXES, None, None)
    return jax.shard_map(body, mesh=mesh, in_specs=(spec,) * 5, out_specs=spec, check_vma=False)
```

```python
import functools
from collections import namedtuple

import jax
import jax.numpy as jnp
from jax import lax
from jax.experimental import pallas as pl
from jax.experimental.pallas import tpu as pltpu
from jax.sharding import PartitionSpec as P

AXES = ("row", "col")
F32, BF16 = jnp.float32, jnp.bfloat16
CHUNKS = 2

MESSAGES = (
    ("g_outer", 1), ("g_partner", 1),
    ("so_outer", CHUNKS), ("so_partner", CHUNKS), ("si_partner", CHUNKS),
    ("b_partner", 1), ("e_outer", 1), ("v_partner", 1),
    ("h_out", CHUNKS), ("wh_out", 1), ("g_in", CHUNKS), ("wg_in", 1),
)
FIRST = {}
for _name, _count in MESSAGES:
    FIRST[_name] = sum(count for _, count in MESSAGES[: len(FIRST)])
TOTAL = sum(count for _, count in MESSAGES)


def scratch_types(order, columns):
    matrix = pltpu.VMEM((order, order), F32)
    chunked = pltpu.VMEM((CHUNKS, order, order // CHUNKS), F32)
    vector = pltpu.VMEM((order, columns), F32)
    pair = pltpu.VMEM((2, order, order), BF16)
    vector_pair = pltpu.VMEM((2, order, columns), BF16)
    types = dict(diag=matrix, l_in=matrix, l_out=matrix, rhs=vector)
    types.update({name: chunked for name in ("s_out", "s_in", "h_mat", "g_mat")})
    types.update({name: vector for name in ("s_b", "e_vec", "v_vec", "wh", "wg", "via")})
    types.update({f"r_{name}": chunked if count > 1 else vector for name, count in MESSAGES})
    types.update({name: pair for name in ("d2", "x2", "y2", "p2", "lin2", "lout2", "sin2", "sout2", "sip2", "in2", "t2", "u2", "k2")})
    types.update(vec2=vector_pair, bp2=vector_pair)
    types.update(load_sem=pltpu.SemaphoreType.DMA((4,)))
    types.update(send_sem=pltpu.SemaphoreType.DMA((TOTAL,)), recv_sem=pltpu.SemaphoreType.DMA((TOTAL,)))
    return types


def kernel(chain, across, names, d_hbm, low_hbm, up_hbm, b_hbm, g_hbm, out_ref, *scratch):
    s = namedtuple("Scratch", names)(*scratch)
    order = s.diag.shape[0]
    width = order // CHUNKS
    place = lax.axis_index("row") * across + lax.axis_index("col")
    odd = lax.rem(place, 2)
    even = odd == 0
    step = 1 - 2 * odd
    inside = (place > 0) & (place < chain - 1)
    edge = (place == 0) | (place == chain - 1)
    deep = (place != 1) & (place != chain - 2)
    shallow = (place == 1) | (place == chain - 2)

    def device(offset):
        index = lax.rem(place + offset * step + chain, chain)
        return (index // across, lax.rem(index, across))

    peers = {"partner": device(1), "outer": device(-1), "out": device(-2), "in": device(2)}
    sent_if = {"partner": None, "outer": inside, "out": inside, "in": deep}
    came_if = {"partner": None, "outer": inside, "out": deep, "in": inside}

    def guarded(condition, action):
        if condition is None:
            action()
        else:
            pl.when(condition)(action)

    def copy(name, src, chunk):
        dst = getattr(s, "r_" + name)
        index = FIRST[name] + chunk
        if dst.ndim == 3:
            dst = dst.at[chunk]
        return pltpu.make_async_remote_copy(
            src_ref=src if src is not None else dst,
            dst_ref=dst,
            send_sem=s.send_sem.at[index],
            recv_sem=s.recv_sem.at[index],
            device_id=peers[name.split("_")[1]],
            device_id_type=pl.DeviceIdType.MESH,
        )

    pending = []

    def send(name, src, chunk=0):
        guarded(sent_if[name.split("_")[1]], lambda: copy(name, src, chunk).start())
        pending.append((name, src, chunk))

    def receive(name, chunk=0):
        guarded(came_if[name.split("_")[1]], lambda: copy(name, None, chunk).wait_recv())

    def load(src, dst, index):
        return pltpu.make_async_copy(src.at[0], dst, s.load_sem.at[index])

    def load_out(act):
        pl.when(inside & even)(lambda: act(load(low_hbm, s.l_out, 1)))
        pl.when(inside & (odd == 1))(lambda: act(load(up_hbm, s.l_out, 1)))

    def load_in(act):
        pl.when(even)(lambda: act(load(up_hbm, s.l_in, 2)))
        pl.when(odd == 1)(lambda: act(load(low_hbm, s.l_in, 2)))

    barrier = pltpu.get_barrier_semaphore()
    for side in ("partner", "outer", "out", "in"):
        guarded(sent_if[side], lambda: pl.semaphore_signal(
            barrier, inc=1, device_id=peers[side], device_id_type=pl.DeviceIdType.MESH))
    load(d_hbm, s.diag, 0).start()
    load_out(lambda c: c.start())
    load_in(lambda c: c.start())
    load(b_hbm, s.rhs, 3).start()

    pl.semaphore_wait(barrier, 1 + jnp.where(inside, 2, 0) + jnp.where(deep, 1, 0))

    send("g_outer", g_hbm.at[0])
    send("g_partner", g_hbm.at[0])

    def zero(*refs):
        for ref in refs:
            ref[...] = jnp.zeros_like(ref)

    pl.when(edge)(lambda: zero(s.l_out, s.r_g_outer, s.r_so_outer, s.r_e_outer, s.r_g_in, s.r_wg_in))
    pl.when(shallow)(lambda: zero(s.r_h_out, s.r_wh_out))

    def cols(chunk):
        return slice(chunk * width, (chunk + 1) * width)

    def put(pair, value, where=slice(None)):
        high = value.astype(BF16)
        pair[0, :, where] = high
        pair[1, :, where] = (value - high.astype(F32)).astype(BF16)

    def dot(left, right):
        return jnp.dot(left, right, preferred_element_type=F32)

    def multiply(left, right, where=slice(None)):
        high, low = right[0, :, where], right[1, :, where]
        return dot(left[0], high) + (dot(left[0], low) + dot(left[1], high))

    def eye(chunk):
        rows = lax.broadcasted_iota(jnp.int32, (order, width), 0)
        return (rows == lax.broadcasted_iota(jnp.int32, (order, width), 1) + chunk * width).astype(F32)

    def mean_diag():
        total = jnp.float32(0.0)
        for c in range(CHUNKS):
            total += jnp.sum(eye(c) * s.diag[:, cols(c)])
        return total / order

    def invert():
        scale = 1.0 / mean_diag()
        for c in range(CHUNKS):
            block = s.diag[:, cols(c)]
            put(s.d2, block, cols(c))
            put(s.x2, (2.0 * eye(c) - block * scale) * scale, cols(c))
        for c in range(CHUNKS):
            put(s.y2, 2.0 * eye(c) - multiply(s.d2, s.x2, cols(c)), cols(c))
        for c in range(CHUNKS):
            put(s.p2, multiply(s.x2, s.y2, cols(c)), cols(c))

    def times(left, vector):
        put(s.vec2, vector)
        return multiply(left, s.vec2)

    load(d_hbm, s.diag, 0).wait()
    invert()
    load_out(lambda c: c.wait())
    put(s.lout2, s.l_out[...])
    for c in range(CHUNKS):
        block = multiply(s.p2, s.lout2, cols(c))
        s.s_out[c] = block
        send("so_outer", s.s_out.at[c], c)
        send("so_partner", s.s_out.at[c], c)
        put(s.sout2, block, cols(c))
    load(b_hbm, s.rhs, 3).wait()
    s.s_b[...] = times(s.p2, s.rhs[...])
    send("b_partner", s.s_b)
    load_in(lambda c: c.wait())
    put(s.lin2, s.l_in[...])
    for c in range(CHUNKS):
        block = multiply(s.p2, s.lin2, cols(c))
        s.s_in[c] = block
        send("si_partner", s.s_in.at[c], c)
        put(s.sin2, block, cols(c))
    receive("g_partner")
    s.e_vec[...] = s.s_b[...] - times(s.sin2, s.r_g_partner[...])
    send("e_outer", s.e_vec)
    receive("g_outer")
    s.v_vec[...] = times(s.sout2, s.r_g_outer[...])
    send("v_partner", s.v_vec)

    for c in range(CHUNKS):
        receive("si_partner", c)
        put(s.sip2, s.r_si_partner[c], cols(c))
        s.diag[:, cols(c)] = s.diag[:, cols(c)] - multiply(s.lin2, s.sip2, cols(c))
    for c in range(CHUNKS):
        receive("so_partner", c)
        put(s.t2, s.r_so_partner[c], cols(c))
        put(s.in2, -multiply(s.lin2, s.t2, cols(c)), cols(c))
    receive("b_partner")
    put(s.bp2, s.r_b_partner[...])
    s.rhs[...] = s.rhs[...] - multiply(s.lin2, s.bp2)
    receive("v_partner")
    s.via[...] = times(s.lin2, s.r_v_partner[...])
    for c in range(CHUNKS):
        receive("so_outer", c)
        put(s.u2, s.r_so_outer[c], cols(c))
        s.diag[:, cols(c)] = s.diag[:, cols(c)] - multiply(s.lout2, s.u2, cols(c))

    invert()
    for c in range(CHUNKS):
        s.h_mat[c] = multiply(s.p2, s.lout2, cols(c))
        send("h_out", s.h_mat.at[c], c)
    s.wh[...] = times(s.p2, s.rhs[...] + s.via[...])
    send("wh_out", s.wh)
    for c in range(CHUNKS):
        put(s.k2, multiply(s.sip2, s.p2, cols(c)), cols(c))
    for c in range(CHUNKS):
        s.g_mat[c] = multiply(s.k2, s.in2, cols(c))
        send("g_in", s.g_mat.at[c], c)
    receive("e_outer")
    s.wg[...] = times(s.k2, s.rhs[...] - times(s.lout2, s.r_e_outer[...])) - s.r_b_partner[...]
    send("wg_in", s.wg)

    for c in range(CHUNKS):
        receive("h_out", c)
        put(s.t2, s.r_h_out[c], cols(c))
        put(s.u2, multiply(s.in2, s.t2, cols(c)), cols(c))
    for c in range(CHUNKS):
        s.diag[:, cols(c)] = s.diag[:, cols(c)] + multiply(s.u2, s.sip2, cols(c))
    receive("wh_out")
    s.rhs[...] = s.rhs[...] - times(s.in2, s.r_wh_out[...] - multiply(s.t2, s.bp2))
    for c in range(CHUNKS):
        receive("g_in", c)
        put(s.t2, s.r_g_in[c], cols(c))
        s.diag[:, cols(c)] = s.diag[:, cols(c)] + multiply(s.lout2, s.t2, cols(c))
    invert()
    receive("wg_in")
    out_ref[...] = times(s.p2, s.rhs[...] + times(s.lout2, s.r_wg_in[...]))

    for name, src, chunk in pending:
        guarded(sent_if[name.split("_")[1]], lambda: copy(name, src, chunk).wait_send())


def body(diagonal, lower, upper, right_side, guess):
    across = lax.axis_size("col")
    chain = lax.axis_size("row") * across
    order, columns = right_side.shape[1:]
    types = scratch_types(order, columns)
    result = pl.pallas_call(
        functools.partial(kernel, chain, across, tuple(types)),
        out_shape=jax.ShapeDtypeStruct((order, columns), F32),
        in_specs=[pl.BlockSpec(memory_space=pl.ANY)] * 5,
        out_specs=pl.BlockSpec(memory_space=pltpu.VMEM),
        scratch_shapes=list(types.values()),
        compiler_params=pltpu.CompilerParams(collective_id=0, has_side_effects=True),
    )(diagonal, lower, upper, right_side, guess)
    return result[None]


def solution(mesh):
    spec = P(AXES, None, None)
    return jax.shard_map(body, mesh=mesh, in_specs=(spec,) * 5, out_specs=spec, check_vma=False)
```
